32 devices in a mesh: tok: 2 (over core), feat: 16 (over z, y, x).
Axes of the slice: x: 2, y: 2, z: 4, core: 2. Of those that a mesh axis runs over, the one named last changes fastest.
Arguments:
- inputs: bfloat16 [8192, 8192], P('feat', 'tok'), may hold values from -6 to 6
- first_weight: bfloat16 [64, 128, 128], P('feat'), may hold values from -0.5 to 0.5
- second_weight: bfloat16 [64, 128, 512], P('feat'), may hold values from -0.5 to 0.5
- third_weight: bfloat16 [64, 512, 128], P('feat'), may hold values from -0.25 to 0.25
- fourth_weight: bfloat16 [64, 128, 128], P('feat'), may hold values from -0.5 to 0.5
- output_grad: bfloat16 [8192, 8192], P(None, ('tok', 'feat')), may hold values from -6 to 6
Outputs:
- layer_out: bfloat16 [8192, 8192], P(None, ('tok', 'feat'))
- input_grad: bfloat16 [8192, 8192], P('feat', 'tok')
- first_grad: float32 [64, 128, 128], P('feat')
- second_grad: float32 [64, 128, 512], P('feat')
- third_grad: float32 [64, 512, 128], P('feat')
- fourth_grad: float32 [64, 128, 128], P('feat')
The draws below stay inside these ranges and needn't reach their ends.
All inputs are finite; a program needn't handle non-finite values.
Results may differ from the reference program's by a relative error of at most 0.0074.
Values may be sent and summed in bfloat16 or wider, within the bound.
No kernel may reach another device: no remote copies, remote signals or barrier semaphores. Data moves between devices by JAX's collectives and lax.ppermute only.
A program may use at most 192 MiB of HBM per device.

```python
import jax
import jax.numpy as jnp
from jax import lax

NB = 64
BS = 128
HB = 512
TOK_DEV = 4096
D = 8192
TOKENS = 8192
N_TOK = 2


def block_scale(key, shape, cuts, low, top_value):
    def one(axis_at, parts):
        steps = jax.random.uniform(jax.random.fold_in(jax.random.fold_in(key, 6), axis_at), (parts,), jnp.float32, low / len(cuts), top_value / len(cuts))
        return jnp.repeat(jnp.exp(steps), shape[axis_at] // parts).reshape((-1,) + (1,) * (len(shape) - axis_at - 1))

    gain = one(*cuts[0])
    for cut in cuts[1:]:
        gain = gain * one(*cut)
    return gain


def scatter_about(own_key, extent, deviation, bound, cuts=(), held_as=jnp.bfloat16):
    entries = deviation * jax.random.normal(own_key, extent, jnp.float32)
    if cuts:
        entries = entries * block_scale(own_key, extent, cuts, -0.22, 0.18)
    return jnp.clip(entries, -bound, bound).astype(held_as)


def setup_inputs(seed: int = 0) -> dict:
    splits = jax.random.split(jax.random.key(seed), 7)
    inputs = scatter_about(splits[0], (D, TOKENS), 1.0, 6.0, ((0, 16), (1, 2)))
    first_weight = scatter_about(splits[1], (NB, BS, BS), BS ** -0.5, 0.5, ((0, 16),))
    second_weight = scatter_about(splits[2], (NB, BS, HB), BS ** -0.5, 0.5, ((0, 16),))
    third_weight = scatter_about(splits[3], (NB, HB, BS), HB ** -0.5, 0.25, ((0, 16),))
    fourth_weight = scatter_about(splits[4], (NB, BS, BS), BS ** -0.5, 0.5, ((0, 16),))
    output_grad = scatter_about(splits[5], (D, TOKENS), 1.0, 6.0, ((1, 32),))
    return {"inputs": inputs, "first_weight": first_weight, "second_weight": second_weight, "third_weight": third_weight, "fourth_weight": fourth_weight, "output_grad": output_grad}


def gelu_tanh(value):
    return jax.nn.gelu(value, approximate=True)

def permute(value):
    count = value.shape[-1]
    return value.reshape(NB, BS // NB, NB, count).transpose(2, 1, 0, 3).reshape(NB, BS, count)

def forward_mul(value, weight):
    return jnp.einsum('bit,bio->bot', value.astype(jnp.float32), weight.astype(jnp.float32))

def backward_mul(grad, weight):
    return jnp.einsum('bot,bio->bit', grad.astype(jnp.float32), weight.astype(jnp.float32))

def outer_sum(value, grad):
    return jnp.einsum('bit,bot->bio', value.astype(jnp.float32), grad.astype(jnp.float32))

def reference(inputs, first_weight, second_weight, third_weight, fourth_weight, output_grad):
    shards = inputs.reshape(NB, BS, N_TOK, TOK_DEV).transpose(2, 0, 1, 3)
    grads = output_grad.reshape(NB, BS, N_TOK, TOK_DEV).transpose(2, 0, 1, 3)
    zeros_square = jnp.zeros((NB, BS, BS), jnp.float32)
    zeros_up = jnp.zeros((NB, BS, HB), jnp.float32)
    zeros_down = jnp.zeros((NB, HB, BS), jnp.float32)

    def step(carry, pair):
        acc_one, acc_two, acc_three, acc_four = carry
        source, out_grad = pair
        first_act = forward_mul(source, first_weight).astype(jnp.bfloat16)
        first_perm = permute(first_act)
        second_pre = forward_mul(first_perm, second_weight).astype(jnp.bfloat16)
        hidden = gelu_tanh(second_pre.astype(jnp.float32)).astype(jnp.bfloat16)
        third_act = forward_mul(hidden, third_weight).astype(jnp.bfloat16)
        third_perm = permute(third_act)
        result = forward_mul(third_perm, fourth_weight).astype(jnp.bfloat16)
        acc_four = acc_four + outer_sum(third_perm, out_grad)
        third_back = permute(backward_mul(out_grad, fourth_weight).astype(jnp.bfloat16))
        acc_three = acc_three + outer_sum(hidden, third_back)
        hidden_grad = backward_mul(third_back, third_weight)
        pre_grad = jax.vjp(gelu_tanh, second_pre.astype(jnp.float32))[1](hidden_grad)[0].astype(jnp.bfloat16)
        acc_two = acc_two + outer_sum(first_perm, pre_grad)
        first_back = permute(backward_mul(pre_grad, second_weight).astype(jnp.bfloat16))
        acc_one = acc_one + outer_sum(source, first_back)
        source_grad = backward_mul(first_back, first_weight).astype(jnp.bfloat16)
        return ((acc_one, acc_two, acc_three, acc_four), (result, source_grad))
    sums, stacked = lax.scan(step, (zeros_square, zeros_up, zeros_down, zeros_square), (shards, grads))
    results, source_grads = stacked
    layer_out = results.transpose(1, 2, 0, 3).reshape(NB * BS, N_TOK * TOK_DEV)
    input_grad = source_grads.transpose(1, 2, 0, 3).reshape(NB * BS, N_TOK * TOK_DEV)
    scale = (TOK_DEV * N_TOK) ** (-0.5)
    return (layer_out, input_grad, sums[0] * scale, sums[1] * scale, sums[2] * scale, sums[3] * scale)
```

```python
import functools

import jax
import jax.numpy as jnp
from jax import lax
from jax.experimental import pallas as pl
from jax.experimental.pallas import tpu as pltpu
from jax.sharding import PartitionSpec as P

BF = jnp.bfloat16
F32 = jnp.float32
CB = 4
TT = 256


def gelu_tanh(value):
    return jax.nn.gelu(value, approximate=True)


def into_raw(source, weight, parts):
    count, in_width, out_width = weight.shape
    shaped = weight.reshape(count, in_width, out_width // (parts * count), parts, count)
    return jnp.einsum("cit,cikdq->dckqt", source, shaped, preferred_element_type=F32)


def from_blocks(grad, weight, parts):
    count, in_width, out_width = weight.shape
    shaped = weight.reshape(count, in_width // (parts * count), parts, count, out_width)
    return jnp.einsum("qot,qksco->sckqt", grad, shaped, preferred_element_type=F32)


def raw_to_blocks(received):
    count = received.shape[1]
    tokens = received.shape[4]
    width = received.shape[0] * count * received.shape[2]
    return jnp.transpose(received, (3, 2, 0, 1, 4)).reshape(count, width, tokens)


def raw_back(received, weight, parts):
    count, in_width, out_width = weight.shape
    shaped = weight.reshape(count, in_width, out_width // (parts * count), parts, count)
    return jnp.einsum("dckqt,cikdq->cit", received, shaped, preferred_element_type=F32)


def raw_outer(source, received):
    count, in_width, _ = source.shape
    out_width = received.shape[0] * received.shape[2] * received.shape[3]
    grad = jnp.einsum("cit,dckqt->cikdq", source, received, preferred_element_type=F32)
    return grad.reshape(count, in_width, out_width)


def local_any(inputs, first_weight, second_weight, third_weight, fourth_weight, output_grad):
    count, width, _ = first_weight.shape
    parts = lax.axis_size("feat")
    blocks_all = count * parts
    tok_dev = inputs.shape[1]
    tok_part = output_grad.shape[1]
    scale = (tok_dev * lax.axis_size("tok")) ** (-0.5)
    source = inputs.reshape(count, width, tok_dev)
    first_raw = into_raw(source, first_weight, parts).astype(BF)
    first_perm = raw_to_blocks(
        lax.all_to_all(first_raw, "feat", split_axis=0, concat_axis=0, tiled=True)
    )
    pre = jnp.einsum("qit,qio->qot", first_perm, second_weight, preferred_element_type=F32).astype(BF)
    act = gelu_tanh(pre.astype(F32)).astype(BF)
    third_raw = into_raw(act, third_weight, parts).astype(BF)
    permuted = raw_to_blocks(
        lax.all_to_all(third_raw, "feat", split_axis=0, concat_axis=0, tiled=True)
    )
    result = jnp.einsum("qit,qio->qot", permuted, fourth_weight, preferred_element_type=F32).astype(BF)
    out_tokens = lax.all_to_all(result, "feat", split_axis=2, concat_axis=0, tiled=True)
    layer_out = out_tokens.reshape(blocks_all * width, tok_part)
    grad_blocks = lax.all_to_all(
        output_grad.reshape(blocks_all, width, tok_part), "feat", split_axis=0, concat_axis=2, tiled=True
    )
    fourth_sum = jnp.einsum("qit,qot->qio", permuted, grad_blocks, preferred_element_type=F32)
    back_raw = from_blocks(grad_blocks, fourth_weight, parts).astype(BF)
    third_back = lax.all_to_all(back_raw, "feat", split_axis=0, concat_axis=0, tiled=True)
    hidden_grad = raw_back(third_back, third_weight, parts)
    third_sum = raw_outer(act, third_back)
    pre_grad = jax.vjp(gelu_tanh, pre.astype(F32))[1](hidden_grad)[0].astype(BF)
    second_sum = jnp.einsum("qit,qot->qio", first_perm, pre_grad, preferred_element_type=F32)
    first_raw_back = from_blocks(pre_grad, second_weight, parts).astype(BF)
    first_back = lax.all_to_all(first_raw_back, "feat", split_axis=0, concat_axis=0, tiled=True)
    first_sum = raw_outer(source, first_back)
    input_grad = raw_back(first_back, first_weight, parts).astype(BF).reshape(count * width, tok_dev)
    totals = lax.psum((first_sum, second_sum, third_sum, fourth_sum), "tok")
    return (layer_out, input_grad) + tuple(total * scale for total in totals)


def rows8(parts):
    return jnp.concatenate([part.astype(F32) for part in parts], axis=0)


def masked(compact):
    wide = jnp.concatenate([compact.astype(F32)] * CB, axis=1)
    row = lax.broadcasted_iota(jnp.int32, wide.shape, 0)
    lane = lax.broadcasted_iota(jnp.int32, wide.shape, 1)
    return jnp.where(row % CB == lane // compact.shape[1], wide, 0.0)


def compacted(wide):
    width = wide.shape[1] // CB
    row = lax.broadcasted_iota(jnp.int32, wide.shape, 0)
    lane = lax.broadcasted_iota(jnp.int32, wide.shape, 1)
    kept = jnp.where(row % CB == lane // width, wide, 0.0)
    return sum(kept[:, c * width : (c + 1) * width] for c in range(CB))


def dot(a, b, a_dim=1, b_dim=0):
    return lax.dot_general(a, b, (((a_dim,), (b_dim,)), ((), ())), preferred_element_type=F32)


def split_kernel(grouping, who, x0, x1, a_ref, *rest):
    outs, big = rest[:8], rest[8]
    f = who[0]

    @pl.when(pl.program_id(0) == 0)
    def _():
        big[...] = masked(jnp.concatenate([a_ref[f ^ r] for r in range(16)], axis=0)).astype(BF)

    for e, x in enumerate((x0, x1)):
        y = dot(big[...], x[...]).astype(BF)
        for r in range(16):
            h, s = e ^ (r >> 3), 8 * e + (r & 7)
            i, j = (s >> 2, s & 3) if grouping[h] == "z" else (s & 3, s >> 2)
            outs[4 * h + i][j, :, 0] = y[32 * r : 32 * r + 32].astype(F32).reshape(4, 8, TT).astype(BF)


def back_kernel(who, og, a_ref, *rest):
    outs = rest
    f, tok = who[0], who[1]
    big = masked(
        jnp.concatenate([a_ref[((f ^ r) >> 3) ^ tok, 0, (f ^ r) & 7] for r in range(16)], axis=0)
    ).astype(BF)
    y = dot(big, og[...])
    for r in range(16):
        outs[r & 7][r >> 3, 0] = y[32 * r : 32 * r + 32].reshape(4, 8, TT).astype(BF)


def middle_kernel(grouping, who, *refs):
    x_near, x_far, tb = refs[:4], refs[4:7], refs[7:15]
    w_ref = refs[15]
    fb_out, ta_out, g_ref = refs[16:20], refs[20:28], refs[28]
    sg, tg = refs[29], refs[30]
    f = who[0]

    def place(s):
        return (s >> 2, s & 3) if grouping == "z" else (s & 3, s >> 2)

    w2f = rows8([w_ref[0, 0, f ^ s] for s in range(16)])
    w2 = w2f.astype(BF)
    w2t = w2f.T.astype(BF)
    w3tf = w_ref[0, 1].astype(F32).reshape(128, w2.shape[1])
    w3t = w3tf.astype(BF)
    w3 = w3tf.T.astype(BF)
    for q in range(8):
        at = (f & 7) ^ q
        pieces = []
        for s in range(16):
            i, j = place(s)
            pieces.append(x_near[i][0, 0, at] if j == 0 else x_far[j - 1][i, 0, at])
        x = rows8(pieces).astype(BF)
        back = tb[q][0, :, 0].astype(F32).reshape(128, TT).astype(BF)
        v = dot(w2t, x).astype(BF).astype(F32)
        hidden_grad = dot(w3, back)
        vv = v * v
        t = jnp.tanh(v * (0.7978845608028654 + (0.7978845608028654 * 0.044715) * vv))
        half = 0.5 + 0.5 * t
        hidden = (v * half).astype(BF)
        slope = half + (0.5 * v) * (1.0 - t * t) * (
            0.7978845608028654 + (3 * 0.7978845608028654 * 0.044715) * vv
        )
        pre_grad = (hidden_grad * slope).astype(BF)
        ta_out[q][:, 0] = dot(w3t, hidden).reshape(16, 8, TT).astype(BF)
        fb = dot(w2, pre_grad)
        for s in range(16):
            i, j = place(s)
            fb_out[i][j, 0, at] = fb[8 * s : 8 * s + 8].astype(BF)
        s_now = dot(x, pre_grad, 1, 1)
        t_now = dot(back, hidden, 1, 1)
        if q == 0:
            sg[...] = s_now
            tg[...] = t_now
        else:
            sg[...] += s_now
            tg[...] += t_now
    total = sg[...]
    for s in range(16):
        g_ref[0, 0, f ^ s] = total[8 * s : 8 * s + 8]
    g_ref[0, 1] = tg[...].reshape(16, 8, -1)


def token_kernel(who, *refs):
    pieces, og, a_ref, out, g_ref = refs[:16], refs[16], refs[17], refs[18], refs[19]
    f, tok = who[0], who[1]
    big = masked(
        jnp.concatenate([a_ref[((f ^ r) >> 3) ^ tok, 0, (f ^ r) & 7] for r in range(16)], axis=0)
    ).astype(BF)
    rows = jnp.concatenate([piece[0].astype(F32).reshape(32, TT) for piece in pieces], axis=0).astype(BF)
    out[...] = dot(big, rows, 0, 0).astype(BF)
    g = compacted(dot(rows, og[...], 1, 1))
    for r in range(16):
        g_ref[((f ^ r) >> 3) ^ tok, 0, (f ^ r) & 7] = g[32 * r : 32 * r + 32]


def finish_kernel(grouping, who, *refs):
    chunks = (refs[:7], refs[7:14])
    x, a_ref, out, g_ref, big, acc = refs[14:20]
    f = who[0]
    e = pl.program_id(0)
    t = pl.program_id(1)

    @pl.when((e == 0) & (t == 0))
    def _():
        big[...] = masked(jnp.concatenate([a_ref[f ^ r] for r in range(16)], axis=0)).T.astype(BF)
        acc[...] = jnp.zeros_like(acc)

    def piece(h, s):
        i, j = (s >> 2, s & 3) if grouping[h] == "z" else (s & 3, s >> 2)
        got = chunks[h][i][0, :, 0] if j == 0 else chunks[h][3 + j][i, :, 0]
        return got.astype(F32).reshape(32, TT)

    def run(half):
        rows = jnp.concatenate(
            [piece(half ^ (r >> 3), 8 * half + (r & 7)) for r in range(16)], axis=0
        ).astype(BF)
        out[...] = dot(big[...], rows).astype(BF)
        acc[...] += dot(rows, x[...], 1, 1)

    @pl.when(e == 0)
    def _():
        run(0)

    @pl.when(e == 1)
    def _():
        run(1)

    @pl.when((e == 1) & (t == pl.num_programs(1) - 1))
    def _():
        g = compacted(acc[...])
        for r in range(16):
            g_ref[f ^ r] = g[32 * r : 32 * r + 32]


def call(kernel, grid, in_specs, out_specs, out_shape, scratch=(), flops=0, bytes_=0):
    return pl.pallas_call(
        kernel,
        grid_spec=pltpu.PrefetchScalarGridSpec(
            num_scalar_prefetch=1, grid=grid, in_specs=in_specs, out_specs=out_specs, scratch_shapes=list(scratch)
        ),
        out_shape=out_shape,
        compiler_params=pltpu.CompilerParams(
            dimension_semantics=("arbitrary",) * len(grid), vmem_limit_bytes=56 * 2**20
        ),
        cost_estimate=pl.CostEstimate(flops=flops, transcendentals=0, bytes_accessed=bytes_),
    )


def shape(dims, dtype=BF):
    return jax.ShapeDtypeStruct(dims, dtype)


def flip(value, bits):
    return lax.ppermute(value, "feat", [(i, i ^ bits) for i in range(16)])


def swap(value):
    return lax.ppermute(value, "tok", [(0, 1), (1, 0)])


def two_stage(groups, first):
    one, two = (4, 1) if first == "z" else (1, 4)
    near = [groups[0]] + [flip(groups[i], one * i) for i in (1, 2, 3)]
    far = [flip(jnp.stack([n[j] for n in near]), two * j) for j in (1, 2, 3)]
    return near + far


def local_halves(inputs, first_weight, second_weight, third_weight, fourth_weight, output_grad):
    count, width, hidden = second_weight.shape
    tok_dev, tok_part = inputs.shape[1], output_grad.shape[1]
    scale = (tok_dev * 2) ** (-0.5)
    tiles = tok_dev // 2 // TT
    f, tok = lax.axis_index("feat"), lax.axis_index("tok")
    who = jnp.stack([f, tok, f >> 3]).astype(jnp.int32)
    grouping = ("xy", "z")
    order = (1, 0)

    a_one = first_weight.reshape(CB, width, 2, 64).transpose(3, 2, 0, 1).reshape(16, 32, width)
    a_four = fourth_weight.reshape(CB, 2, 64, width).transpose(2, 1, 0, 3).reshape(2, 8, 32, width)
    w_two = second_weight.reshape(CB, 2, 16, CB, hidden).transpose(0, 2, 1, 3, 4).reshape(CB, 16, 8, hidden)
    w_three = third_weight.reshape(CB, hidden, 2, 16, CB).transpose(0, 3, 2, 4, 1).reshape(CB, 16, 8, hidden)
    w_own = jnp.stack([w_two, w_three], axis=1)

    got = lax.dynamic_slice_in_dim(a_four, tok, 1, 0)
    for bits in (8, 4, 2, 1):
        got = jnp.concatenate([got, flip(got, bits)], axis=0)
    got = got.reshape(2, 2, 2, 2, 8, 32, width).transpose(3, 2, 1, 0, 4, 5, 6).reshape(16, 8, 32, width)
    a_all = jnp.stack([got, swap(got)])

    w_half = flip(lax.dynamic_slice_in_dim(w_own, 2 * tok, 2, 0), 8)
    w_far = jnp.concatenate([w_half, swap(w_half)], axis=0)

    tile_specs = [pl.BlockSpec((512, TT), lambda t, w, e=e: (0, (w[2] ^ e) * tiles + t)) for e in (0, 1)]
    whole_a = pl.BlockSpec((16, 32, width), lambda t, w: (0, 0, 0))
    group = shape((4, 4, tiles, 8, TT))
    sent = call(
        functools.partial(split_kernel, grouping), (tiles,),
        tile_specs + [whole_a],
        [pl.BlockSpec((4, 4, 1, 8, TT), lambda t, w: (0, 0, t, 0, 0))] * 8,
        [group] * 8,
        [pltpu.VMEM((512, 512), BF)],
        2 * 512 * 512 * tok_dev, 4 * 512 * tok_dev,
    )(who, inputs, inputs, a_one)
    arrived = {h: two_stage(sent[4 * h : 4 * h + 4], grouping[h]) for h in order}

    a_spec = pl.BlockSpec((2, 1, 8, 32, width), lambda n, w: (0, n, 0, 0, 0))
    og_spec = pl.BlockSpec((512, TT), lambda n, w: (w[0] ^ n, 0))
    back = call(
        back_kernel, (16,), [og_spec, a_spec],
        [pl.BlockSpec((2, 1, 4, 8, TT), lambda n, w: (0, w[0] ^ n, 0, 0, 0))] * 8,
        [shape((2, 16, 4, 8, TT))] * 8, (), 2 * 512 * 8192 * TT, 4 * 8192 * TT,
    )(who, output_grad, a_all)
    back = [back[0]] + [flip(back[s], s) for s in range(1, 8)]

    results = {}
    near_spec = pl.BlockSpec((1, 1, tiles, 8, TT), lambda l, w: (0, l, 0, 0, 0))
    far_spec = pl.BlockSpec((4, 1, tiles, 8, TT), lambda l, w: (0, l, 0, 0, 0))
    rows_spec = pl.BlockSpec((16, 1, 8, TT), lambda l, w: (0, l, 0, 0))
    for h in order:
        back_spec = pl.BlockSpec((1, 16, 1, 8, TT), lambda l, w, h=h: (h, 0, l, 0, 0))
        w_spec = pl.BlockSpec((1, 2, 16, 8, hidden), lambda l, w, h=h: (l ^ (2 * w[1] * h), 0, 0, 0, 0))
        g_spec = pl.BlockSpec((1, 2, 16, 8, hidden), lambda l, w: (l ^ (2 * w[1]), 0, 0, 0, 0))
        results[h] = call(
            functools.partial(middle_kernel, grouping[h]), (4,),
            [near_spec] * 4 + [far_spec] * 3 + [back_spec] * 8 + [w_spec],
            [far_spec] * 4 + [rows_spec] * 8 + [g_spec],
            [group] * 4 + [shape((16, 4, 8, TT))] * 8 + [shape((4, 2, 16, 8, hidden), F32)],
            [pltpu.VMEM((128, hidden), F32)] * 2,
            12 * 4 * 128 * hidden * tok_dev // 2, 20 * 2**20,
        )(who, *arrived[h], *back, w_far if h else w_own)
    returned = {h: two_stage(results[h][:4], grouping[h]) for h in order}
    acts = {h: [results[h][4]] + [flip(results[h][4 + s], s) for s in range(1, 8)] for h in order}

    near_spec = pl.BlockSpec((1, 4, 1, 8, TT), lambda e, t, w: (0, 0, t, 0, 0))
    far_spec = pl.BlockSpec((4, 4, 1, 8, TT), lambda e, t, w: (0, 0, t, 0, 0))
    tile_spec = pl.BlockSpec((512, TT), lambda e, t, w: (0, (w[2] ^ e) * tiles + t))
    whole_a = pl.BlockSpec((16, 32, width), lambda e, t, w: (0, 0, 0))
    input_grad, first = call(
        functools.partial(finish_kernel, grouping), (2, tiles),
        ([near_spec] * 4 + [far_spec] * 3) * 2 + [tile_spec, whole_a],
        [tile_spec, whole_a],
        [shape((512, tok_dev)), shape((16, 32, width), F32)],
        [pltpu.VMEM((512, 512), BF), pltpu.VMEM((512, 512), F32)],
        4 * 512 * 512 * tok_dev, 6 * 512 * tok_dev,
    )(who, *returned[0], *returned[1], inputs, a_one)

    layer_out, fourth = call(
        token_kernel, (16,),
        [pl.BlockSpec((1, 4, 8, TT), lambda n, w: (w[0] ^ n, 0, 0, 0))] * 16 + [og_spec, a_spec],
        [og_spec, a_spec],
        [shape((8192, tok_part)), shape((2, 16, 8, 32, width), F32)], (),
        4 * 512 * 8192 * TT, 6 * 8192 * TT,
    )(who, *acts[0], *acts[1], output_grad, a_all)

    def both(mine):
        other = swap(mine)
        low, high = jnp.where(tok == 0, mine, other), jnp.where(tok == 0, other, mine)
        return jnp.concatenate([low, high], axis=0)

    kept = [results[h][12][:2] + swap(results[h][12][2:].astype(BF)).astype(F32) for h in (0, 1)]
    middle = both(kept[0] + flip(kept[1].astype(BF), 8).astype(F32)) * scale
    second = middle[:, 0].reshape(CB, 16, 2, CB, hidden).transpose(0, 2, 1, 3, 4).reshape(CB, width, hidden)
    third = middle[:, 1].reshape(CB, 16, 2, CB, hidden).transpose(0, 4, 2, 1, 3).reshape(CB, hidden, width)

    part = fourth[0] + swap(fourth[1].astype(BF)).astype(F32)
    for low in (1, 2, 4, 8):
        pairs = part.reshape(-1, 2, 8, 32, width)
        part = pairs[:, 0] + flip(pairs[:, 1].astype(BF), low).astype(F32)
    fourth = both(part[0]).reshape(16, CB, 2, CB, width) * scale
    fourth = fourth.transpose(3, 2, 0, 1, 4).reshape(CB, width, width)

    first = (first + swap(first)).reshape(16, CB, 2, CB, width) * scale
    first = first.transpose(3, 4, 2, 0, 1).reshape(CB, width, width)
    return (layer_out, input_grad, first, second, third, fourth)


def solution(mesh):
    placed = (
        P("feat", "tok"),
        P("feat", None, None),
        P("feat", None, None),
        P("feat", None, None),
        P("feat", None, None),
        P(None, ("tok", "feat")),
    )

    def local(inputs, first_weight, second_weight, third_weight, fourth_weight, output_grad):
        fits = (
            mesh.shape["feat"] == 16
            and mesh.shape["tok"] == 2
            and first_weight.shape == (CB, 128, 128)
            and output_grad.shape == (8192, TT)
            and inputs.shape[1] == 16 * TT
        )
        run = local_halves if fits else local_any
        return run(inputs, first_weight, second_weight, third_weight, fourth_weight, output_grad)

    return jax.shard_map(
        local,
        mesh=mesh,
        in_specs=placed,
        out_specs=(
            P(None, ("tok", "feat")),
            P("feat", "tok"),
            P("feat", None, None),
            P("feat", None, None),
            P("feat", None, None),
            P("feat", None, None),
        ),
        check_vma=False,
    )
```

```python
import functools

import jax
import jax.numpy as jnp
from jax import lax
from jax.experimental import pallas as pl
from jax.experimental.pallas import tpu as pltpu
from jax.sharding import PartitionSpec as P

BF = jnp.bfloat16
F32 = jnp.float32
CB = 4
TT = 256
STEP = 4
PAIR = 2


def gelu_tanh(value):
    return jax.nn.gelu(value, approximate=True)


def into_raw(source, weight, parts):
    count, in_width, out_width = weight.shape
    shaped = weight.reshape(count, in_width, out_width // (parts * count), parts, count)
    return jnp.einsum("cit,cikdq->dckqt", source, shaped, preferred_element_type=F32)


def from_blocks(grad, weight, parts):
    count, in_width, out_width = weight.shape
    shaped = weight.reshape(count, in_width // (parts * count), parts, count, out_width)
    return jnp.einsum("qot,qksco->sckqt", grad, shaped, preferred_element_type=F32)


def raw_to_blocks(received):
    count = received.shape[1]
    tokens = received.shape[4]
    width = received.shape[0] * count * received.shape[2]
    return jnp.transpose(received, (3, 2, 0, 1, 4)).reshape(count, width, tokens)


def raw_back(received, weight, parts):
    count, in_width, out_width = weight.shape
    shaped = weight.reshape(count, in_width, out_width // (parts * count), parts, count)
    return jnp.einsum("dckqt,cikdq->cit", received, shaped, preferred_element_type=F32)


def raw_outer(source, received):
    count, in_width, _ = source.shape
    out_width = received.shape[0] * received.shape[2] * received.shape[3]
    grad = jnp.einsum("cit,dckqt->cikdq", source, received, preferred_element_type=F32)
    return grad.reshape(count, in_width, out_width)


def local_any(inputs, first_weight, second_weight, third_weight, fourth_weight, output_grad):
    count, width, _ = first_weight.shape
    parts = lax.axis_size("feat")
    blocks_all = count * parts
    tok_dev = inputs.shape[1]
    tok_part = output_grad.shape[1]
    scale = (tok_dev * lax.axis_size("tok")) ** (-0.5)
    source = inputs.reshape(count, width, tok_dev)
    first_raw = into_raw(source, first_weight, parts).astype(BF)
    first_perm = raw_to_blocks(
        lax.all_to_all(first_raw, "feat", split_axis=0, concat_axis=0, tiled=True)
    )
    pre = jnp.einsum("qit,qio->qot", first_perm, second_weight, preferred_element_type=F32).astype(BF)
    act = gelu_tanh(pre.astype(F32)).astype(BF)
    third_raw = into_raw(act, third_weight, parts).astype(BF)
    permuted = raw_to_blocks(
        lax.all_to_all(third_raw, "feat", split_axis=0, concat_axis=0, tiled=True)
    )
    result = jnp.einsum("qit,qio->qot", permuted, fourth_weight, preferred_element_type=F32).astype(BF)
    out_tokens = lax.all_to_all(result, "feat", split_axis=2, concat_axis=0, tiled=True)
    layer_out = out_tokens.reshape(blocks_all * width, tok_part)
    grad_blocks = lax.all_to_all(
        output_grad.reshape(blocks_all, width, tok_part), "feat", split_axis=0, concat_axis=2, tiled=True
    )
    fourth_sum = jnp.einsum("qit,qot->qio", permuted, grad_blocks, preferred_element_type=F32)
    back_raw = from_blocks(grad_blocks, fourth_weight, parts).astype(BF)
    third_back = lax.all_to_all(back_raw, "feat", split_axis=0, concat_axis=0, tiled=True)
    hidden_grad = raw_back(third_back, third_weight, parts)
    third_sum = raw_outer(act, third_back)
    pre_grad = jax.vjp(gelu_tanh, pre.astype(F32))[1](hidden_grad)[0].astype(BF)
    second_sum = jnp.einsum("qit,qot->qio", first_perm, pre_grad, preferred_element_type=F32)
    first_raw_back = from_blocks(pre_grad, second_weight, parts).astype(BF)
    first_back = lax.all_to_all(first_raw_back, "feat", split_axis=0, concat_axis=0, tiled=True)
    first_sum = raw_outer(source, first_back)
    input_grad = raw_back(first_back, first_weight, parts).astype(BF).reshape(count * width, tok_dev)
    totals = lax.psum((first_sum, second_sum, third_sum, fourth_sum), "tok")
    return (layer_out, input_grad) + tuple(total * scale for total in totals)


def rows8(parts):
    return jnp.concatenate([part.astype(F32) for part in parts], axis=0)


def masked(compact):
    rows, width = compact.shape
    wide = compact.astype(F32)
    row = lax.broadcasted_iota(jnp.int32, (rows, width), 0) % CB
    return jnp.concatenate([jnp.where(row == c, wide, 0.0) for c in range(CB)], axis=1)


def compacted(wide):
    rows, width = wide.shape[0], wide.shape[1] // CB
    row = lax.broadcasted_iota(jnp.int32, (rows, width), 0) % CB
    kept = wide[:, :width]
    for c in range(1, CB):
        kept = jnp.where(row == c, wide[:, c * width : (c + 1) * width], kept)
    return kept


def dot(a, b, a_dim=1, b_dim=0):
    return lax.dot_general(a, b, (((a_dim,), (b_dim,)), ((), ())), preferred_element_type=F32)


def split_kernel(grouping, who, x0, x1, a_ref, *rest):
    outs, big = rest[:8], rest[8]
    f = who[0]

    @pl.when(pl.program_id(0) == 0)
    def _():
        big[...] = masked(jnp.concatenate([a_ref[f ^ r] for r in range(16)], axis=0)).astype(BF)

    for e, x in enumerate((x0, x1)):
        for n in range(PAIR):
            y = dot(big[...], x[:, TT * n : TT * n + TT])
            for r in range(16):
                h, s = e ^ (r >> 3), 8 * e + (r & 7)
                i, j = (s >> 2, s & 3) if grouping[h] == "z" else (s & 3, s >> 2)
                outs[4 * h + i][j, :, n] = y[32 * r : 32 * r + 32].reshape(4, 8, TT).astype(BF)


def gathered(who, a_ref, n):
    f, tok = who[0], who[1]
    rows = [a_ref[((f ^ r) >> 3) ^ tok, n, (f ^ r) & 7] for r in range(16)]
    return masked(jnp.concatenate(rows, axis=0)).astype(BF)


def group_rows(at):
    return pl.ds(pl.multiple_of(512 * at, 512), 512)


def back_kernel(who, og, a_ref, *outs):
    for n in range(STEP):
        at = (who[0] & (STEP - 1)) ^ n
        y = dot(gathered(who, a_ref, n), og[group_rows(at), :])
        for r in range(16):
            outs[r >> 3][(who[0] & 7) ^ (r & 7), at] = y[32 * r : 32 * r + 32].reshape(4, 8, TT).astype(BF)


def middle_kernel(grouping, who, *refs):
    x_near, x_far, tb, w_ref = refs[:4], refs[4:7], refs[7], refs[8]
    fb_out, ta_out, g_ref = refs[9:13], refs[13], refs[14]
    sg, tg = refs[15], refs[16]
    f = who[0]

    def place(s):
        return (s >> 2, s & 3) if grouping == "z" else (s & 3, s >> 2)

    w2f = rows8([w_ref[0, 0, f ^ s] for s in range(16)])
    w2 = w2f.astype(BF)
    w2t = w2f.T.astype(BF)
    w3tf = w_ref[0, 1].astype(F32).reshape(128, w2.shape[1])
    w3t = w3tf.astype(BF)
    w3 = w3tf.T.astype(BF)
    for q in range(8):
        at = (f & 7) ^ q
        pieces = []
        for s in range(16):
            i, j = place(s)
            pieces.append(x_near[i][0, 0, at] if j == 0 else x_far[j - 1][i, 0, at])
        x = rows8(pieces).astype(BF)
        back = tb[at, :, 0].astype(F32).reshape(128, TT).astype(BF)
        v = dot(w2t, x).astype(BF).astype(F32)
        hidden_grad = dot(w3, back)
        vv = v * v
        t = jnp.tanh(v * (0.7978845608028654 + (0.7978845608028654 * 0.044715) * vv))
        half = 0.5 + 0.5 * t
        hidden = (v * half).astype(BF)
        slope = half + (0.5 * v) * (1.0 - t * t) * (
            0.7978845608028654 + (3 * 0.7978845608028654 * 0.044715) * vv
        )
        pre_grad = (hidden_grad * slope).astype(BF)
        ta_out[at, :, 0] = dot(w3t, hidden).reshape(16, 8, TT).astype(BF)
        fb = dot(w2, pre_grad)
        for s in range(16):
            i, j = place(s)
            fb_out[i][j, 0, at] = fb[8 * s : 8 * s + 8].astype(BF)
        s_now = dot(x, pre_grad, 1, 1)
        t_now = dot(back, hidden, 1, 1)
        if q == 0:
            sg[...] = s_now
            tg[...] = t_now
        else:
            sg[...] += s_now
            tg[...] += t_now
    total = sg[...]
    for s in range(16):
        g_ref[0, 0, f ^ s] = total[8 * s : 8 * s + 8]
    g_ref[0, 1] = tg[...].reshape(16, 8, -1)


def token_kernel(who, *refs):
    pieces, og, a_ref, out, g_ref = refs[:2], refs[2], refs[3], refs[4], refs[5]
    f, tok = who[0], who[1]
    for n in range(STEP):
        at = (f & (STEP - 1)) ^ n
        parts = [pieces[r >> 3][(f & 7) ^ (r & 7), at] for r in range(16)]
        rows = jnp.concatenate([part.astype(F32).reshape(32, TT) for part in parts], axis=0).astype(BF)
        out[group_rows(at), :] = dot(gathered(who, a_ref, n), rows, 0, 0).astype(BF)
        g = compacted(dot(rows, og[group_rows(at), :], 1, 1))
        for r in range(16):
            g_ref[((f ^ r) >> 3) ^ tok, n, (f ^ r) & 7] = g[32 * r : 32 * r + 32]


def finish_kernel(grouping, who, *refs):
    chunks = (refs[:7], refs[7:14])
    x, a_ref, out, g_ref, big, acc = refs[14:20]
    f = who[0]
    e = pl.program_id(0)
    t = pl.program_id(1)

    @pl.when((e == 0) & (t == 0))
    def _():
        big[...] = masked(jnp.concatenate([a_ref[f ^ r] for r in range(16)], axis=0)).T.astype(BF)
        acc[...] = jnp.zeros_like(acc)

    def piece(h, s, n):
        i, j = (s >> 2, s & 3) if grouping[h] == "z" else (s & 3, s >> 2)
        got = chunks[h][i][0, :, n] if j == 0 else chunks[h][3 + j][i, :, n]
        return got.astype(F32).reshape(32, TT)

    def run(half):
        rows = jnp.concatenate(
            [
                jnp.concatenate([piece(half ^ (r >> 3), 8 * half + (r & 7), n) for n in range(PAIR)], axis=1)
                for r in range(16)
            ],
            axis=0,
        ).astype(BF)
        out[...] = dot(big[...], rows).astype(BF)
        acc[...] += dot(rows, x[...], 1, 1)

    @pl.when(e == 0)
    def _():
        run(0)

    @pl.when(e == 1)
    def _():
        run(1)

    @pl.when((e == 1) & (t == pl.num_programs(1) - 1))
    def _():
        g = compacted(acc[...])
        for r in range(16):
            g_ref[f ^ r] = g[32 * r : 32 * r + 32]


def call(kernel, grid, in_specs, out_specs, out_shape, scratch=(), flops=0, bytes_=0):
    return pl.pallas_call(
        kernel,
        grid_spec=pltpu.PrefetchScalarGridSpec(
            num_scalar_prefetch=1, grid=grid, in_specs=in_specs, out_specs=out_specs, scratch_shapes=list(scratch)
        ),
        out_shape=out_shape,
        compiler_params=pltpu.CompilerParams(
            dimension_semantics=("arbitrary",) * len(grid), vmem_limit_bytes=56 * 2**20
        ),
        cost_estimate=pl.CostEstimate(flops=flops, transcendentals=0, bytes_accessed=bytes_),
    )


def shape(dims, dtype=BF):
    return jax.ShapeDtypeStruct(dims, dtype)


def flip(value, bits):
    return lax.ppermute(value, "feat", [(i, i ^ bits) for i in range(16)])


def spread(value):
    groups = [list(range(8)), list(range(8, 16))]
    return lax.all_to_all(value, "feat", 0, 0, axis_index_groups=groups, tiled=True)


def swap(value):
    return lax.ppermute(value, "tok", [(0, 1), (1, 0)])


def two_stage(groups, first):
    one, two = (4, 1) if first == "z" else (1, 4)
    near = [groups[0]] + [flip(groups[i], one * i) for i in (1, 2, 3)]
    far = [flip(jnp.stack([n[j] for n in near]), two * j) for j in (1, 2, 3)]
    return near + far


def local_halves(inputs, first_weight, second_weight, third_weight, fourth_weight, output_grad):
    _, width, hidden = second_weight.shape
    tok_dev, tok_part = inputs.shape[1], output_grad.shape[1]
    scale = (tok_dev * 2) ** (-0.5)
    tiles = tok_dev // 2 // TT
    steps = tiles // PAIR
    f, tok = lax.axis_index("feat"), lax.axis_index("tok")
    who = jnp.stack([f, tok, f >> 3]).astype(jnp.int32)
    grouping = ("xy", "z")
    order = (1, 0)

    a_one = first_weight.reshape(CB, width, 2, 64).transpose(3, 2, 0, 1).reshape(16, 32, width)
    a_four = fourth_weight.reshape(CB, 2, 64, width).transpose(2, 1, 0, 3).reshape(2, 8, 32, width)
    w_two = second_weight.reshape(CB, 2, 16, CB, hidden).transpose(0, 2, 1, 3, 4).reshape(CB, 16, 8, hidden)
    w_three = third_weight.reshape(CB, hidden, 2, 16, CB).transpose(0, 3, 2, 4, 1).reshape(CB, 16, 8, hidden)
    w_own = jnp.stack([w_two, w_three], axis=1)

    got = lax.dynamic_slice_in_dim(a_four, tok, 1, 0)
    got = jnp.concatenate([got] + [flip(got, bits) for bits in (4, 8, 12)], axis=0)
    got = [got] + [flip(got, bits) for bits in (1, 2, 3)]
    got = jnp.stack(got, axis=1).reshape(16, 8, 32, width)
    a_all = jnp.stack([got, swap(got)])

    w_half = flip(lax.dynamic_slice_in_dim(w_own, 2 * tok, 2, 0), 8)
    w_far = jnp.concatenate([w_half, swap(w_half)], axis=0)

    tile_specs = [pl.BlockSpec((512, PAIR * TT), lambda t, w, e=e: (0, (w[2] ^ e) * steps + t)) for e in (0, 1)]
    whole_a = pl.BlockSpec((16, 32, width), lambda t, w: (0, 0, 0))
    group = shape((4, 4, tiles, 8, TT))
    sent = call(
        functools.partial(split_kernel, grouping), (steps,),
        tile_specs + [whole_a],
        [pl.BlockSpec((4, 4, PAIR, 8, TT), lambda t, w: (0, 0, t, 0, 0))] * 8,
        [group] * 8,
        [pltpu.VMEM((512, 512), BF)],
        2 * 512 * 512 * tok_dev, 4 * 512 * tok_dev,
    )(who, inputs, inputs, a_one)
    arrived = {h: two_stage(sent[4 * h : 4 * h + 4], grouping[h]) for h in order}

    a_spec = pl.BlockSpec((2, STEP, 8, 32, width), lambda n, w: (0, n, 0, 0, 0))
    og_spec = pl.BlockSpec((512 * STEP, TT), lambda n, w: ((w[0] // STEP) ^ n, 0))
    back = call(
        back_kernel, (16 // STEP,), [og_spec, a_spec],
        [pl.BlockSpec((8, STEP, 4, 8, TT), lambda n, w: (0, (w[0] // STEP) ^ n, 0, 0, 0))] * 2,
        [shape((8, 16, 4, 8, TT))] * 2, (), 2 * 512 * 8192 * TT, 4 * 8192 * TT,
    )(who, output_grad, a_all)
    back = {h: spread(back[h]) for h in order}

    results = {}
    near_spec = pl.BlockSpec((1, 1, tiles, 8, TT), lambda l, w: (0, l, 0, 0, 0))
    far_spec = pl.BlockSpec((4, 1, tiles, 8, TT), lambda l, w: (0, l, 0, 0, 0))
    rows_spec = pl.BlockSpec((8, 16, 1, 8, TT), lambda l, w: (0, 0, l, 0, 0))
    for h in order:
        w_spec = pl.BlockSpec((1, 2, 16, 8, hidden), lambda l, w, h=h: (l ^ (2 * w[1] * h), 0, 0, 0, 0))
        g_spec = pl.BlockSpec((1, 2, 16, 8, hidden), lambda l, w: (l ^ (2 * w[1]), 0, 0, 0, 0))
        results[h] = call(
            functools.partial(middle_kernel, grouping[h]), (4,),
            [near_spec] * 4 + [far_spec] * 3 + [rows_spec, w_spec],
            [far_spec] * 4 + [rows_spec, g_spec],
            [group] * 4 + [shape((8, 16, 4, 8, TT))] + [shape((4, 2, 16, 8, hidden), F32)],
            [pltpu.VMEM((128, hidden), F32)] * 2,
            12 * 4 * 128 * hidden * tok_dev // 2, 20 * 2**20,
        )(who, *arrived[h], back[h], w_far if h else w_own)
    returned = {h: two_stage(results[h][:4], grouping[h]) for h in order}
    acts = {h: spread(results[h][4]) for h in order}

    near_spec = pl.BlockSpec((1, 4, PAIR, 8, TT), lambda e, t, w: (0, 0, t, 0, 0))
    far_spec = pl.BlockSpec((4, 4, PAIR, 8, TT), lambda e, t, w: (0, 0, t, 0, 0))
    tile_spec = pl.BlockSpec((512, PAIR * TT), lambda e, t, w: (0, (w[2] ^ e) * steps + t))
    whole_a = pl.BlockSpec((16, 32, width), lambda e, t, w: (0, 0, 0))
    input_grad, first = call(
        functools.partial(finish_kernel, grouping), (2, steps),
        ([near_spec] * 4 + [far_spec] * 3) * 2 + [tile_spec, whole_a],
        [tile_spec, whole_a],
        [shape((512, tok_dev)), shape((16, 32, width), F32)],
        [pltpu.VMEM((512, 512), BF), pltpu.VMEM((512, 512), F32)],
        4 * 512 * 512 * tok_dev, 6 * 512 * tok_dev,
    )(who, *returned[0], *returned[1], inputs, a_one)

    layer_out, fourth = call(
        token_kernel, (16 // STEP,),
        [pl.BlockSpec((8, STEP, 4, 8, TT), lambda n, w: (0, (w[0] // STEP) ^ n, 0, 0, 0))] * 2 + [og_spec, a_spec],
        [og_spec, a_spec],
        [shape((8192, tok_part)), shape((2, 16, 8, 32, width), F32)], (),
        4 * 512 * 8192 * TT, 6 * 8192 * TT,
    )(who, acts[0], acts[1], output_grad, a_all)

    def both(mine):
        other = swap(mine)
        low, high = jnp.where(tok == 0, mine, other), jnp.where(tok == 0, other, mine)
        return jnp.concatenate([low, high], axis=0)

    kept = [results[h][5][:2] + swap(results[h][5][2:].astype(BF)).astype(F32) for h in (0, 1)]
    middle = both(kept[0] + flip(kept[1].astype(BF), 8).astype(F32)) * scale
    second = middle[:, 0].reshape(CB, 16, 2, CB, hidden).transpose(0, 2, 1, 3, 4).reshape(CB, width, hidden)
    third = middle[:, 1].reshape(CB, 16, 2, CB, hidden).transpose(0, 4, 2, 1, 3).reshape(CB, hidden, width)

    part = fourth[0] + swap(fourth[1].astype(BF)).astype(F32)
    part = part.reshape(4, 4, 8, 32, width)
    part = part[:, 0] + sum(flip(part[:, j].astype(BF), j).astype(F32) for j in (1, 2, 3))
    part = part[0] + sum(flip(part[j].astype(BF), 4 * j).astype(F32) for j in (1, 2, 3))
    fourth = both(part).reshape(16, CB, 2, CB, width) * scale
    fourth = fourth.transpose(3, 2, 0, 1, 4).reshape(CB, width, width)

    first = (first + swap(first)).reshape(16, CB, 2, CB, width) * scale
    first = first.transpose(3, 4, 2, 0, 1).reshape(CB, width, width)
    return (layer_out, input_grad, first, second, third, fourth)


def solution(mesh):
    placed = (
        P("feat", "tok"),
        P("feat", None, None),
        P("feat", None, None),
        P("feat", None, None),
        P("feat", None, None),
        P(None, ("tok", "feat")),
    )

    def local(inputs, first_weight, second_weight, third_weight, fourth_weight, output_grad):
        fits = (
            mesh.shape["feat"] == 16
            and mesh.shape["tok"] == 2
            and first_weight.shape == (CB, 128, 128)
            and output_grad.shape == (8192, TT)
            and inputs.shape[1] == 16 * TT
        )
        run = local_halves if fits else local_any
        return run(inputs, first_weight, second_weight, third_weight, fourth_weight, output_grad)

    return jax.shard_map(
        local,
        mesh=mesh,
        in_specs=placed,
        out_specs=(
            P(None, ("tok", "feat")),
            P("feat", "tok"),
            P("feat", None, None),
            P("feat", None, None),
            P("feat", None, None),
            P("feat", None, None),
        ),
        check_vma=False,
    )
```

```python
import functools

import jax
import jax.numpy as jnp
from jax import lax
from jax.experimental import pallas as pl
from jax.experimental.pallas import tpu as pltpu
from jax.sharding import PartitionSpec as P

BF = jnp.bfloat16
F32 = jnp.float32
CB = 4
TT = 256
STEP = 4
PAIR = 2

GO = ("z", "xy")
COME = ("z", "z")


def gelu_tanh(value):
    return jax.nn.gelu(value, approximate=True)


def into_raw(source, weight, parts):
    count, in_width, out_width = weight.shape
    shaped = weight.reshape(count, in_width, out_width // (parts * count), parts, count)
    return jnp.einsum("cit,cikdq->dckqt", source, shaped, preferred_element_type=F32)


def from_blocks(grad, weight, parts):
    count, in_width, out_width = weight.shape
    shaped = weight.reshape(count, in_width // (parts * count), parts, count, out_width)
    return jnp.einsum("qot,qksco->sckqt", grad, shaped, preferred_element_type=F32)


def raw_to_blocks(received):
    count = received.shape[1]
    tokens = received.shape[4]
    width = received.shape[0] * count * received.shape[2]
    return jnp.transpose(received, (3, 2, 0, 1, 4)).reshape(count, width, tokens)


def raw_back(received, weight, parts):
    count, in_width, out_width = weight.shape
    shaped = weight.reshape(count, in_width, out_width // (parts * count), parts, count)
    return jnp.einsum("dckqt,cikdq->cit", received, shaped, preferred_element_type=F32)


def raw_outer(source, received):
    count, in_width, _ = source.shape
    out_width = received.shape[0] * received.shape[2] * received.shape[3]
    grad = jnp.einsum("cit,dckqt->cikdq", source, received, preferred_element_type=F32)
    return grad.reshape(count, in_width, out_width)


def local_any(inputs, first_weight, second_weight, third_weight, fourth_weight, output_grad):
    count, width, _ = first_weight.shape
    parts = lax.axis_size("feat")
    blocks_all = count * parts
    tok_dev = inputs.shape[1]
    tok_part = output_grad.shape[1]
    scale = (tok_dev * lax.axis_size("tok")) ** (-0.5)
    source = inputs.reshape(count, width, tok_dev)
    first_raw = into_raw(source, first_weight, parts).astype(BF)
    first_perm = raw_to_blocks(
        lax.all_to_all(first_raw, "feat", split_axis=0, concat_axis=0, tiled=True)
    )
    pre = jnp.einsum("qit,qio->qot", first_perm, second_weight, preferred_element_type=F32).astype(BF)
    act = gelu_tanh(pre.astype(F32)).astype(BF)
    third_raw = into_raw(act, third_weight, parts).astype(BF)
    permuted = raw_to_blocks(
        lax.all_to_all(third_raw, "feat", split_axis=0, concat_axis=0, tiled=True)
    )
    result = jnp.einsum("qit,qio->qot", permuted, fourth_weight, preferred_element_type=F32).astype(BF)
    out_tokens = lax.all_to_all(result, "feat", split_axis=2, concat_axis=0, tiled=True)
    layer_out = out_tokens.reshape(blocks_all * width, tok_part)
    grad_blocks = lax.all_to_all(
        output_grad.reshape(blocks_all, width, tok_part), "feat", split_axis=0, concat_axis=2, tiled=True
    )
    fourth_sum = jnp.einsum("qit,qot->qio", permuted, grad_blocks, preferred_element_type=F32)
    back_raw = from_blocks(grad_blocks, fourth_weight, parts).astype(BF)
    third_back = lax.all_to_all(back_raw, "feat", split_axis=0, concat_axis=0, tiled=True)
    hidden_grad = raw_back(third_back, third_weight, parts)
    third_sum = raw_outer(act, third_back)
    pre_grad = jax.vjp(gelu_tanh, pre.astype(F32))[1](hidden_grad)[0].astype(BF)
    second_sum = jnp.einsum("qit,qot->qio", first_perm, pre_grad, preferred_element_type=F32)
    first_raw_back = from_blocks(pre_grad, second_weight, parts).astype(BF)
    first_back = lax.all_to_all(first_raw_back, "feat", split_axis=0, concat_axis=0, tiled=True)
    first_sum = raw_outer(source, first_back)
    input_grad = raw_back(first_back, first_weight, parts).astype(BF).reshape(count * width, tok_dev)
    totals = lax.psum((first_sum, second_sum, third_sum, fourth_sum), "tok")
    return (layer_out, input_grad) + tuple(total * scale for total in totals)


def rows8(parts):
    return jnp.concatenate([part.astype(F32) for part in parts], axis=0)


def masked(compact):
    rows, width = compact.shape
    wide = compact.astype(F32)
    row = lax.broadcasted_iota(jnp.int32, (rows, width), 0) % CB
    return jnp.concatenate([jnp.where(row == c, wide, 0.0) for c in range(CB)], axis=1)


def compacted(wide):
    rows, width = wide.shape[0], wide.shape[1] // CB
    row = lax.broadcasted_iota(jnp.int32, (rows, width), 0) % CB
    kept = wide[:, :width]
    for c in range(1, CB):
        kept = jnp.where(row == c, wide[:, c * width : (c + 1) * width], kept)
    return kept


def dot(a, b, a_dim=1, b_dim=0):
    return lax.dot_general(a, b, (((a_dim,), (b_dim,)), ((), ())), preferred_element_type=F32)


def split_kernel(grouping, who, x0, x1, a_ref, *rest):
    outs, big = rest[:8], rest[8]
    f = who[0]

    @pl.when(pl.program_id(0) == 0)
    def _():
        big[...] = masked(jnp.concatenate([a_ref[f ^ r] for r in range(16)], axis=0)).astype(BF)

    for e, x in enumerate((x0, x1)):
        for n in range(PAIR):
            y = dot(big[...], x[:, TT * n : TT * n + TT])
            for r in range(16):
                h, s = e ^ (r >> 3), 8 * e + (r & 7)
                i, j = (s >> 2, s & 3) if grouping[h] == "z" else (s & 3, s >> 2)
                outs[4 * h + i][j, :, n] = y[32 * r : 32 * r + 32].reshape(4, 8, TT).astype(BF)


def gathered(who, a_ref, n):
    f, tok = who[0], who[1]
    rows = [a_ref[((f ^ r) >> 3) ^ tok, n, (f ^ r) & 7] for r in range(16)]
    return masked(jnp.concatenate(rows, axis=0)).astype(BF)


def group_rows(at):
    return pl.ds(pl.multiple_of(512 * at, 512), 512)


def back_kernel(who, og, a_ref, *outs):
    for n in range(STEP):
        at = (who[0] & (STEP - 1)) ^ n
        y = dot(gathered(who, a_ref, n), og[group_rows(at), :])
        for r in range(16):
            outs[r >> 3][(who[0] & 7) ^ (r & 7), at] = y[32 * r : 32 * r + 32].reshape(4, 8, TT).astype(BF)


def middle_kernel(go, come, who, *refs):
    x_near, x_far, tb, w_ref = refs[:4], refs[4:7], refs[7], refs[8]
    fb_out, ta_out, g_ref = refs[9:13], refs[13:21], refs[21]
    sg, tg = refs[22], refs[23]
    f = who[0]

    def place(s, first):
        return (s >> 2, s & 3) if first == "z" else (s & 3, s >> 2)

    w2f = rows8([w_ref[0, 0, f ^ s] for s in range(16)])
    w2 = w2f.astype(BF)
    w2t = w2f.T.astype(BF)
    w3tf = w_ref[0, 1].astype(F32).reshape(128, w2.shape[1])
    w3t = w3tf.astype(BF)
    w3 = w3tf.T.astype(BF)
    for q in range(8):
        at = (f & 7) ^ q
        pieces = []
        for s in range(16):
            i, j = place(s, go)
            pieces.append(x_near[i][0, 0, at] if j == 0 else x_far[j - 1][i, 0, at])
        x = rows8(pieces).astype(BF)
        back = tb[at, :, 0].astype(F32).reshape(128, TT).astype(BF)
        v = dot(w2t, x).astype(BF).astype(F32)
        hidden_grad = dot(w3, back)
        vv = v * v
        t = jnp.tanh(v * (0.7978845608028654 + (0.7978845608028654 * 0.044715) * vv))
        half = 0.5 + 0.5 * t
        hidden = (v * half).astype(BF)
        slope = half + (0.5 * v) * (1.0 - t * t) * (
            0.7978845608028654 + (3 * 0.7978845608028654 * 0.044715) * vv
        )
        pre_grad = (hidden_grad * slope).astype(BF)
        ta_out[q][:, 0] = dot(w3t, hidden).reshape(16, 8, TT).astype(BF)
        fb = dot(w2, pre_grad)
        for s in range(16):
            i, j = place(s, come)
            fb_out[i][j, 0, at] = fb[8 * s : 8 * s + 8].astype(BF)
        s_now = dot(x, pre_grad, 1, 1)
        t_now = dot(back, hidden, 1, 1)
        if q == 0:
            sg[...] = s_now
            tg[...] = t_now
        else:
            sg[...] += s_now
            tg[...] += t_now
    total = sg[...]
    for s in range(16):
        g_ref[0, 0, f ^ s] = total[8 * s : 8 * s + 8]
    g_ref[0, 1] = tg[...].reshape(16, 8, -1)


def token_kernel(who, *refs):
    pieces, og, a_ref, out, g_ref = refs[:16], refs[16], refs[17], refs[18], refs[19]
    f, tok = who[0], who[1]
    for n in range(STEP):
        at = (f & (STEP - 1)) ^ n
        parts = [piece[at] for piece in pieces]
        rows = jnp.concatenate([part.astype(F32).reshape(32, TT) for part in parts], axis=0).astype(BF)
        out[group_rows(at), :] = dot(gathered(who, a_ref, n), rows, 0, 0).astype(BF)
        g = compacted(dot(rows, og[group_rows(at), :], 1, 1))
        for r in range(16):
            g_ref[((f ^ r) >> 3) ^ tok, n, (f ^ r) & 7] = g[32 * r : 32 * r + 32]


def finish_kernel(grouping, who, *refs):
    chunks = (refs[:7], refs[7:14])
    x, a_ref, out, g_ref, big, acc = refs[14:20]
    f = who[0]
    e = pl.program_id(0)
    t = pl.program_id(1)

    @pl.when((e == 0) & (t == 0))
    def _():
        big[...] = masked(jnp.concatenate([a_ref[f ^ r] for r in range(16)], axis=0)).T.astype(BF)
        acc[...] = jnp.zeros_like(acc)

    def piece(h, s, n):
        i, j = (s >> 2, s & 3) if grouping[h] == "z" else (s & 3, s >> 2)
        got = chunks[h][i][0, :, n] if j == 0 else chunks[h][3 + j][i, :, n]
        return got.astype(F32).reshape(32, TT)

    def run(half):
        rows = jnp.concatenate(
            [
                jnp.concatenate([piece(half ^ (r >> 3), 8 * half + (r & 7), n) for n in range(PAIR)], axis=1)
                for r in range(16)
            ],
            axis=0,
        ).astype(BF)
        out[...] = dot(big[...], rows).astype(BF)
        acc[...] += dot(rows, x[...], 1, 1)

    @pl.when(e == 0)
    def _():
        run(0)

    @pl.when(e == 1)
    def _():
        run(1)

    @pl.when((e == 1) & (t == pl.num_programs(1) - 1))
    def _():
        g = compacted(acc[...])
        for r in range(16):
            g_ref[f ^ r] = g[32 * r : 32 * r + 32]


def call(kernel, grid, in_specs, out_specs, out_shape, scratch=(), flops=0, bytes_=0):
    return pl.pallas_call(
        kernel,
        grid_spec=pltpu.PrefetchScalarGridSpec(
            num_scalar_prefetch=1, grid=grid, in_specs=in_specs, out_specs=out_specs, scratch_shapes=list(scratch)
        ),
        out_shape=out_shape,
        compiler_params=pltpu.CompilerParams(
            dimension_semantics=("arbitrary",) * len(grid), vmem_limit_bytes=56 * 2**20
        ),
        cost_estimate=pl.CostEstimate(flops=flops, transcendentals=0, bytes_accessed=bytes_),
    )


def shape(dims, dtype=BF):
    return jax.ShapeDtypeStruct(dims, dtype)


def flip(value, bits):
    return lax.ppermute(value, "feat", [(i, i ^ bits) for i in range(16)])


def spread(value):
    groups = [list(range(8)), list(range(8, 16))]
    return lax.all_to_all(value, "feat", 0, 0, axis_index_groups=groups, tiled=True)


def swap(value):
    return lax.ppermute(value, "tok", [(0, 1), (1, 0)])


def two_stage(groups, first):
    one, two = (4, 1) if first == "z" else (1, 4)
    near = [groups[0]] + [flip(groups[i], one * i) for i in (1, 2, 3)]
    far = [flip(jnp.stack([n[j] for n in near]), two * j) for j in (1, 2, 3)]
    return near + far


def local_halves(inputs, first_weight, second_weight, third_weight, fourth_weight, output_grad):
    _, width, hidden = second_weight.shape
    tok_dev, tok_part = inputs.shape[1], output_grad.shape[1]
    scale = (tok_dev * 2) ** (-0.5)
    tiles = tok_dev // 2 // TT
    steps = tiles // PAIR
    f, tok = lax.axis_index("feat"), lax.axis_index("tok")
    who = jnp.stack([f, tok, f >> 3]).astype(jnp.int32)
    order = (0, 1)

    a_one = first_weight.reshape(CB, width, 2, 64).transpose(3, 2, 0, 1).reshape(16, 32, width)
    a_four = fourth_weight.reshape(CB, 2, 64, width).transpose(2, 1, 0, 3).reshape(2, 8, 32, width)
    w_two = second_weight.reshape(CB, 2, 16, CB, hidden).transpose(0, 2, 1, 3, 4).reshape(CB, 16, 8, hidden)
    w_three = third_weight.reshape(CB, hidden, 2, 16, CB).transpose(0, 3, 2, 4, 1).reshape(CB, 16, 8, hidden)
    w_own = jnp.stack([w_two, w_three], axis=1)

    got = lax.dynamic_slice_in_dim(a_four, tok, 1, 0)
    got = jnp.concatenate([got] + [flip(got, bits) for bits in (4, 8, 12)], axis=0)
    got = [got] + [flip(got, bits) for bits in (1, 2, 3)]
    got = jnp.stack(got, axis=1).reshape(16, 8, 32, width)
    a_all = jnp.stack([got, swap(got)])

    w_half = flip(lax.dynamic_slice_in_dim(w_own, 2 * tok, 2, 0), 8)
    w_far = jnp.concatenate([w_half, swap(w_half)], axis=0)

    tile_specs = [pl.BlockSpec((512, PAIR * TT), lambda t, w, e=e: (0, (w[2] ^ e) * steps + t)) for e in (0, 1)]
    whole_a = pl.BlockSpec((16, 32, width), lambda t, w: (0, 0, 0))
    group = shape((4, 4, tiles, 8, TT))
    sent = call(
        functools.partial(split_kernel, GO), (steps,),
        tile_specs + [whole_a],
        [pl.BlockSpec((4, 4, PAIR, 8, TT), lambda t, w: (0, 0, t, 0, 0))] * 8,
        [group] * 8,
        [pltpu.VMEM((512, 512), BF)],
        2 * 512 * 512 * tok_dev, 4 * 512 * tok_dev,
    )(who, inputs, inputs, a_one)
    arrived = {h: two_stage(sent[4 * h : 4 * h + 4], GO[h]) for h in order}

    a_spec = pl.BlockSpec((2, STEP, 8, 32, width), lambda n, w: (0, n, 0, 0, 0))
    og_spec = pl.BlockSpec((512 * STEP, TT), lambda n, w: ((w[0] // STEP) ^ n, 0))
    back = call(
        back_kernel, (16 // STEP,), [og_spec, a_spec],
        [pl.BlockSpec((8, STEP, 4, 8, TT), lambda n, w: (0, (w[0] // STEP) ^ n, 0, 0, 0))] * 2,
        [shape((8, 16, 4, 8, TT))] * 2, (), 2 * 512 * 8192 * TT, 4 * 8192 * TT,
    )(who, output_grad, a_all)
    back = {h: spread(back[h]) for h in order}

    results = {}
    near_spec = pl.BlockSpec((1, 1, tiles, 8, TT), lambda l, w: (0, l, 0, 0, 0))
    far_spec = pl.BlockSpec((4, 1, tiles, 8, TT), lambda l, w: (0, l, 0, 0, 0))
    act_spec = pl.BlockSpec((16, 1, 8, TT), lambda l, w: (0, l, 0, 0))
    rows_spec = pl.BlockSpec((8, 16, 1, 8, TT), lambda l, w: (0, 0, l, 0, 0))
    for h in order:
        w_spec = pl.BlockSpec((1, 2, 16, 8, hidden), lambda l, w, h=h: (l ^ (2 * w[1] * h), 0, 0, 0, 0))
        g_spec = pl.BlockSpec((1, 2, 16, 8, hidden), lambda l, w: (l ^ (2 * w[1]), 0, 0, 0, 0))
        results[h] = call(
            functools.partial(middle_kernel, GO[h], COME[h]), (4,),
            [near_spec] * 4 + [far_spec] * 3 + [rows_spec, w_spec],
            [far_spec] * 4 + [act_spec] * 8 + [g_spec],
            [group] * 4 + [shape((16, 4, 8, TT))] * 8 + [shape((4, 2, 16, 8, hidden), F32)],
            [pltpu.VMEM((128, hidden), F32)] * 2,
            12 * 4 * 128 * hidden * tok_dev // 2, 20 * 2**20,
        )(who, *arrived[h], back[h], w_far if h else w_own)
    returned = {h: two_stage(results[h][:4], COME[h]) for h in order}
    acts = {h: [results[h][4]] + [flip(results[h][4 + s], s) for s in range(1, 8)] for h in order}

    near_spec = pl.BlockSpec((1, 4, PAIR, 8, TT), lambda e, t, w: (0, 0, t, 0, 0))
    far_spec = pl.BlockSpec((4, 4, PAIR, 8, TT), lambda e, t, w: (0, 0, t, 0, 0))
    tile_spec = pl.BlockSpec((512, PAIR * TT), lambda e, t, w: (0, (w[2] ^ e) * steps + t))
    whole_a = pl.BlockSpec((16, 32, width), lambda e, t, w: (0, 0, 0))
    input_grad, first = call(
        functools.partial(finish_kernel, COME), (2, steps),
        ([near_spec] * 4 + [far_spec] * 3) * 2 + [tile_spec, whole_a],
        [tile_spec, whole_a],
        [shape((512, tok_dev)), shape((16, 32, width), F32)],
        [pltpu.VMEM((512, 512), BF), pltpu.VMEM((512, 512), F32)],
        4 * 512 * 512 * tok_dev, 6 * 512 * tok_dev,
    )(who, *returned[0], *returned[1], inputs, a_one)

    layer_out, fourth = call(
        token_kernel, (16 // STEP,),
        [pl.BlockSpec((STEP, 4, 8, TT), lambda n, w: ((w[0] // STEP) ^ n, 0, 0, 0))] * 16 + [og_spec, a_spec],
        [og_spec, a_spec],
        [shape((8192, tok_part)), shape((2, 16, 8, 32, width), F32)], (),
        4 * 512 * 8192 * TT, 6 * 8192 * TT,
    )(who, *acts[0], *acts[1], output_grad, a_all)

    def both(mine):
        other = swap(mine)
        low, high = jnp.where(tok == 0, mine, other), jnp.where(tok == 0, other, mine)
        return jnp.concatenate([low, high], axis=0)

    kept = [results[h][12][:2] + swap(results[h][12][2:].astype(BF)).astype(F32) for h in (0, 1)]
    middle = both(kept[0] + flip(kept[1].astype(BF), 8).astype(F32)) * scale
    second = middle[:, 0].reshape(CB, 16, 2, CB, hidden).transpose(0, 2, 1, 3, 4).reshape(CB, width, hidden)
    third = middle[:, 1].reshape(CB, 16, 2, CB, hidden).transpose(0, 4, 2, 1, 3).reshape(CB, hidden, width)

    part = fourth[0] + swap(fourth[1].astype(BF)).astype(F32)
    part = part.reshape(4, 4, 8, 32, width)
    part = part[:, 0] + sum(flip(part[:, j].astype(BF), j).astype(F32) for j in (1, 2, 3))
    part = part[0] + sum(flip(part[j].astype(BF), 4 * j).astype(F32) for j in (1, 2, 3))
    fourth = both(part).reshape(16, CB, 2, CB, width) * scale
    fourth = fourth.transpose(3, 2, 0, 1, 4).reshape(CB, width, width)

    first = (first + swap(first)).reshape(16, CB, 2, CB, width) * scale
    first = first.transpose(3, 4, 2, 0, 1).reshape(CB, width, width)
    return (layer_out, input_grad, first, second, third, fourth)


def solution(mesh):
    placed = (
        P("feat", "tok"),
        P("feat", None, None),
        P("feat", None, None),
        P("feat", None, None),
        P("feat", None, None),
        P(None, ("tok", "feat")),
    )

    def local(inputs, first_weight, second_weight, third_weight, fourth_weight, output_grad):
        fits = (
            mesh.shape["feat"] == 16
            and mesh.shape["tok"] == 2
            and first_weight.shape == (CB, 128, 128)
            and output_grad.shape == (8192, TT)
            and inputs.shape[1] == 16 * TT
        )
        run = local_halves if fits else local_any
        return run(inputs, first_weight, second_weight, third_weight, fourth_weight, output_grad)

    return jax.shard_map(
        local,
        mesh=mesh,
        in_specs=placed,
        out_specs=(
            P(None, ("tok", "feat")),
            P("feat", "tok"),
            P("feat", None, None),
            P("feat", None, None),
            P("feat", None, None),
            P("feat", None, None),
        ),
        check_vma=False,
    )
```

```python
import functools

import jax
import jax.numpy as jnp
from jax import lax
from jax.experimental import pallas as pl
from jax.experimental.pallas import tpu as pltpu
from jax.sharding import PartitionSpec as P

BF = jnp.bfloat16
F32 = jnp.float32
CB = 4
TT = 256
STEP = 4
PAIR = 2

GO = ("z", "xy")
COME = ("z", "xy")


def gelu_tanh(value):
    return jax.nn.gelu(value, approximate=True)


def into_raw(source, weight, parts):
    count, in_width, out_width = weight.shape
    shaped = weight.reshape(count, in_width, out_width // (parts * count), parts, count)
    return jnp.einsum("cit,cikdq->dckqt", source, shaped, preferred_element_type=F32)


def from_blocks(grad, weight, parts):
    count, in_width, out_width = weight.shape
    shaped = weight.reshape(count, in_width // (parts * count), parts, count, out_width)
    return jnp.einsum("qot,qksco->sckqt", grad, shaped, preferred_element_type=F32)


def raw_to_blocks(received):
    count = received.shape[1]
    tokens = received.shape[4]
    width = received.shape[0] * count * received.shape[2]
    return jnp.transpose(received, (3, 2, 0, 1, 4)).reshape(count, width, tokens)


def raw_back(received, weight, parts):
    count, in_width, out_width = weight.shape
    shaped = weight.reshape(count, in_width, out_width // (parts * count), parts, count)
    return jnp.einsum("dckqt,cikdq->cit", received, shaped, preferred_element_type=F32)


def raw_outer(source, received):
    count, in_width, _ = source.shape
    out_width = received.shape[0] * received.shape[2] * received.shape[3]
    grad = jnp.einsum("cit,dckqt->cikdq", source, received, preferred_element_type=F32)
    return grad.reshape(count, in_width, out_width)


def local_any(inputs, first_weight, second_weight, third_weight, fourth_weight, output_grad):
    count, width, _ = first_weight.shape
    parts = lax.axis_size("feat")
    blocks_all = count * parts
    tok_dev = inputs.shape[1]
    tok_part = output_grad.shape[1]
    scale = (tok_dev * lax.axis_size("tok")) ** (-0.5)
    source = inputs.reshape(count, width, tok_dev)
    first_raw = into_raw(source, first_weight, parts).astype(BF)
    first_perm = raw_to_blocks(
        lax.all_to_all(first_raw, "feat", split_axis=0, concat_axis=0, tiled=True)
    )
    pre = jnp.einsum("qit,qio->qot", first_perm, second_weight, preferred_element_type=F32).astype(BF)
    act = gelu_tanh(pre.astype(F32)).astype(BF)
    third_raw = into_raw(act, third_weight, parts).astype(BF)
    permuted = raw_to_blocks(
        lax.all_to_all(third_raw, "feat", split_axis=0, concat_axis=0, tiled=True)
    )
    result = jnp.einsum("qit,qio->qot", permuted, fourth_weight, preferred_element_type=F32).astype(BF)
    out_tokens = lax.all_to_all(result, "feat", split_axis=2, concat_axis=0, tiled=True)
    layer_out = out_tokens.reshape(blocks_all * width, tok_part)
    grad_blocks = lax.all_to_all(
        output_grad.reshape(blocks_all, width, tok_part), "feat", split_axis=0, concat_axis=2, tiled=True
    )
    fourth_sum = jnp.einsum("qit,qot->qio", permuted, grad_blocks, preferred_element_type=F32)
    back_raw = from_blocks(grad_blocks, fourth_weight, parts).astype(BF)
    third_back = lax.all_to_all(back_raw, "feat", split_axis=0, concat_axis=0, tiled=True)
    hidden_grad = raw_back(third_back, third_weight, parts)
    third_sum = raw_outer(act, third_back)
    pre_grad = jax.vjp(gelu_tanh, pre.astype(F32))[1](hidden_grad)[0].astype(BF)
    second_sum = jnp.einsum("qit,qot->qio", first_perm, pre_grad, preferred_element_type=F32)
    first_raw_back = from_blocks(pre_grad, second_weight, parts).astype(BF)
    first_back = lax.all_to_all(first_raw_back, "feat", split_axis=0, concat_axis=0, tiled=True)
    first_sum = raw_outer(source, first_back)
    input_grad = raw_back(first_back, first_weight, parts).astype(BF).reshape(count * width, tok_dev)
    totals = lax.psum((first_sum, second_sum, third_sum, fourth_sum), "tok")
    return (layer_out, input_grad) + tuple(total * scale for total in totals)


def rows8(parts):
    return jnp.concatenate([part.astype(F32) for part in parts], axis=0)


def masked(compact):
    rows, width = compact.shape
    wide = compact.astype(F32)
    row = lax.broadcasted_iota(jnp.int32, (rows, width), 0) % CB
    return jnp.concatenate([jnp.where(row == c, wide, 0.0) for c in range(CB)], axis=1)


def compacted(wide):
    rows, width = wide.shape[0], wide.shape[1] // CB
    row = lax.broadcasted_iota(jnp.int32, (rows, width), 0) % CB
    kept = wide[:, :width]
    for c in range(1, CB):
        kept = jnp.where(row == c, wide[:, c * width : (c + 1) * width], kept)
    return kept


def dot(a, b, a_dim=1, b_dim=0):
    return lax.dot_general(a, b, (((a_dim,), (b_dim,)), ((), ())), preferred_element_type=F32)


def split_kernel(grouping, who, x0, x1, a_ref, *rest):
    outs, big = rest[:8], rest[8]
    f = who[0]

    @pl.when(pl.program_id(0) == 0)
    def _():
        big[...] = masked(jnp.concatenate([a_ref[f ^ r] for r in range(16)], axis=0)).astype(BF)

    for e, x in enumerate((x0, x1)):
        for n in range(PAIR):
            y = dot(big[...], x[:, TT * n : TT * n + TT])
            for r in range(16):
                h, s = e ^ (r >> 3), 8 * e + (r & 7)
                i, j = (s >> 2, s & 3) if grouping[h] == "z" else (s & 3, s >> 2)
                outs[4 * h + i][j, :, n] = y[32 * r : 32 * r + 32].reshape(4, 8, TT).astype(BF)


def gathered(who, a_ref, n):
    f, tok = who[0], who[1]
    rows = [a_ref[((f ^ r) >> 3) ^ tok, n, (f ^ r) & 7] for r in range(16)]
    return masked(jnp.concatenate(rows, axis=0)).astype(BF)


def group_rows(at):
    return pl.ds(pl.multiple_of(512 * at, 512), 512)


def back_kernel(who, og, a_ref, *outs):
    for n in range(STEP):
        at = (who[0] & (STEP - 1)) ^ n
        y = dot(gathered(who, a_ref, n), og[group_rows(at), :])
        for r in range(16):
            outs[r >> 3][(who[0] & 7) ^ (r & 7), at] = y[32 * r : 32 * r + 32].reshape(4, 8, TT).astype(BF)


def middle_kernel(go, come, who, *refs):
    x_near, x_far, tb, w_ref = refs[:4], refs[4:7], refs[7], refs[8]
    fb_out, ta_out, g_ref = refs[9:13], refs[13], refs[14]
    sg, tg = refs[15], refs[16]
    f = who[0]

    def place(s, first):
        return (s >> 2, s & 3) if first == "z" else (s & 3, s >> 2)

    w2f = rows8([w_ref[0, 0, f ^ s] for s in range(16)])
    w2 = w2f.astype(BF)
    w2t = w2f.T.astype(BF)
    w3tf = w_ref[0, 1].astype(F32).reshape(128, w2.shape[1])
    w3t = w3tf.astype(BF)
    w3 = w3tf.T.astype(BF)
    for q in range(8):
        at = (f & 7) ^ q
        pieces = []
        for s in range(16):
            i, j = place(s, go)
            pieces.append(x_near[i][0, 0, at] if j == 0 else x_far[j - 1][i, 0, at])
        x = rows8(pieces).astype(BF)
        back = tb[at, :, 0].astype(F32).reshape(128, TT).astype(BF)
        v = dot(w2t, x).astype(BF).astype(F32)
        hidden_grad = dot(w3, back)
        vv = v * v
        t = jnp.tanh(v * (0.7978845608028654 + (0.7978845608028654 * 0.044715) * vv))
        half = 0.5 + 0.5 * t
        hidden = (v * half).astype(BF)
        slope = half + (0.5 * v) * (1.0 - t * t) * (
            0.7978845608028654 + (3 * 0.7978845608028654 * 0.044715) * vv
        )
        pre_grad = (hidden_grad * slope).astype(BF)
        ta_out[at, :, 0] = dot(w3t, hidden).reshape(16, 8, TT).astype(BF)
        fb = dot(w2, pre_grad)
        for s in range(16):
            i, j = place(s, come)
            fb_out[i][j, 0, at] = fb[8 * s : 8 * s + 8].astype(BF)
        s_now = dot(x, pre_grad, 1, 1)
        t_now = dot(back, hidden, 1, 1)
        if q == 0:
            sg[...] = s_now
            tg[...] = t_now
        else:
            sg[...] += s_now
            tg[...] += t_now
    total = sg[...]
    for s in range(16):
        g_ref[0, 0, f ^ s] = total[8 * s : 8 * s + 8]
    g_ref[0, 1] = tg[...].reshape(16, 8, -1)


def token_kernel(who, *refs):
    pieces, og, a_ref, out, g_ref = refs[:2], refs[2], refs[3], refs[4], refs[5]
    f, tok = who[0], who[1]
    for n in range(STEP):
        at = (f & (STEP - 1)) ^ n
        parts = [pieces[r >> 3][(f & 7) ^ (r & 7), at] for r in range(16)]
        rows = jnp.concatenate([part.astype(F32).reshape(32, TT) for part in parts], axis=0).astype(BF)
        out[group_rows(at), :] = dot(gathered(who, a_ref, n), rows, 0, 0).astype(BF)
        g = compacted(dot(rows, og[group_rows(at), :], 1, 1))
        for r in range(16):
            g_ref[((f ^ r) >> 3) ^ tok, n, (f ^ r) & 7] = g[32 * r : 32 * r + 32]


def finish_kernel(grouping, who, *refs):
    chunks = (refs[:7], refs[7:14])
    x, a_ref, out, g_ref, big, acc = refs[14:20]
    f = who[0]
    e = pl.program_id(0)
    t = pl.program_id(1)

    @pl.when((e == 0) & (t == 0))
    def _():
        big[...] = masked(jnp.concatenate([a_ref[f ^ r] for r in range(16)], axis=0)).T.astype(BF)
        acc[...] = jnp.zeros_like(acc)

    def piece(h, s, n):
        i, j = (s >> 2, s & 3) if grouping[h] == "z" else (s & 3, s >> 2)
        got = chunks[h][i][0, :, n] if j == 0 else chunks[h][3 + j][i, :, n]
        return got.astype(F32).reshape(32, TT)

    def run(half):
        rows = jnp.concatenate(
            [
                jnp.concatenate([piece(half ^ (r >> 3), 8 * half + (r & 7), n) for n in range(PAIR)], axis=1)
                for r in range(16)
            ],
            axis=0,
        ).astype(BF)
        out[...] = dot(big[...], rows).astype(BF)
        acc[...] += dot(rows, x[...], 1, 1)

    @pl.when(e == 0)
    def _():
        run(0)

    @pl.when(e == 1)
    def _():
        run(1)

    @pl.when((e == 1) & (t == pl.num_programs(1) - 1))
    def _():
        g = compacted(acc[...])
        for r in range(16):
            g_ref[f ^ r] = g[32 * r : 32 * r + 32]


def call(kernel, grid, in_specs, out_specs, out_shape, scratch=(), flops=0, bytes_=0):
    return pl.pallas_call(
        kernel,
        grid_spec=pltpu.PrefetchScalarGridSpec(
            num_scalar_prefetch=1, grid=grid, in_specs=in_specs, out_specs=out_specs, scratch_shapes=list(scratch)
        ),
        out_shape=out_shape,
        compiler_params=pltpu.CompilerParams(
            dimension_semantics=("arbitrary",) * len(grid), vmem_limit_bytes=56 * 2**20
        ),
        cost_estimate=pl.CostEstimate(flops=flops, transcendentals=0, bytes_accessed=bytes_),
    )


def shape(dims, dtype=BF):
    return jax.ShapeDtypeStruct(dims, dtype)


def flip(value, bits):
    return lax.ppermute(value, "feat", [(i, i ^ bits) for i in range(16)])


def spread(value):
    groups = [list(range(8)), list(range(8, 16))]
    return lax.all_to_all(value, "feat", 0, 0, axis_index_groups=groups, tiled=True)


def swap(value):
    return lax.ppermute(value, "tok", [(0, 1), (1, 0)])


def two_stage(groups, first):
    one, two = (4, 1) if first == "z" else (1, 4)
    near = [groups[0]] + [flip(groups[i], one * i) for i in (1, 2, 3)]
    far = [flip(jnp.stack([n[j] for n in near]), two * j) for j in (1, 2, 3)]
    return near + far


def local_halves(inputs, first_weight, second_weight, third_weight, fourth_weight, output_grad):
    _, width, hidden = second_weight.shape
    tok_dev, tok_part = inputs.shape[1], output_grad.shape[1]
    scale = (tok_dev * 2) ** (-0.5)
    tiles = tok_dev // 2 // TT
    steps = tiles // PAIR
    f, tok = lax.axis_index("feat"), lax.axis_index("tok")
    who = jnp.stack([f, tok, f >> 3]).astype(jnp.int32)
    order = (0, 1)

    a_one = first_weight.reshape(CB, width, 2, 64).transpose(3, 2, 0, 1).reshape(16, 32, width)
    a_four = fourth_weight.reshape(CB, 2, 64, width).transpose(2, 1, 0, 3).reshape(2, 8, 32, width)
    w_two = second_weight.reshape(CB, 2, 16, CB, hidden).transpose(0, 2, 1, 3, 4).reshape(CB, 16, 8, hidden)
    w_three = third_weight.reshape(CB, hidden, 2, 16, CB).transpose(0, 3, 2, 4, 1).reshape(CB, 16, 8, hidden)
    w_own = jnp.stack([w_two, w_three], axis=1)

    got = lax.dynamic_slice_in_dim(a_four, tok, 1, 0)
    got = jnp.concatenate([got] + [flip(got, bits) for bits in (4, 8, 12)], axis=0)
    got = [got] + [flip(got, bits) for bits in (1, 2, 3)]
    got = jnp.stack(got, axis=1).reshape(16, 8, 32, width)
    a_all = jnp.stack([got, swap(got)])

    w_half = flip(lax.dynamic_slice_in_dim(w_own, 2 * tok, 2, 0), 8)
    w_far = jnp.concatenate([w_half, swap(w_half)], axis=0)

    tile_specs = [pl.BlockSpec((512, PAIR * TT), lambda t, w, e=e: (0, (w[2] ^ e) * steps + t)) for e in (0, 1)]
    whole_a = pl.BlockSpec((16, 32, width), lambda t, w: (0, 0, 0))
    group = shape((4, 4, tiles, 8, TT))
    sent = call(
        functools.partial(split_kernel, GO), (steps,),
        tile_specs + [whole_a],
        [pl.BlockSpec((4, 4, PAIR, 8, TT), lambda t, w: (0, 0, t, 0, 0))] * 8,
        [group] * 8,
        [pltpu.VMEM((512, 512), BF)],
        2 * 512 * 512 * tok_dev, 4 * 512 * tok_dev,
    )(who, inputs, inputs, a_one)
    arrived = {h: two_stage(sent[4 * h : 4 * h + 4], GO[h]) for h in order}

    a_spec = pl.BlockSpec((2, STEP, 8, 32, width), lambda n, w: (0, n, 0, 0, 0))
    og_spec = pl.BlockSpec((512 * STEP, TT), lambda n, w: ((w[0] // STEP) ^ n, 0))
    back = call(
        back_kernel, (16 // STEP,), [og_spec, a_spec],
        [pl.BlockSpec((8, STEP, 4, 8, TT), lambda n, w: (0, (w[0] // STEP) ^ n, 0, 0, 0))] * 2,
        [shape((8, 16, 4, 8, TT))] * 2, (), 2 * 512 * 8192 * TT, 4 * 8192 * TT,
    )(who, output_grad, a_all)
    back = {h: spread(back[h]) for h in order}

    results = {}
    near_spec = pl.BlockSpec((1, 1, tiles, 8, TT), lambda l, w: (0, l, 0, 0, 0))
    far_spec = pl.BlockSpec((4, 1, tiles, 8, TT), lambda l, w: (0, l, 0, 0, 0))
    rows_spec = pl.BlockSpec((8, 16, 1, 8, TT), lambda l, w: (0, 0, l, 0, 0))
    for h in order:
        w_spec = pl.BlockSpec((1, 2, 16, 8, hidden), lambda l, w, h=h: (l ^ (2 * w[1] * h), 0, 0, 0, 0))
        g_spec = pl.BlockSpec((1, 2, 16, 8, hidden), lambda l, w: (l ^ (2 * w[1]), 0, 0, 0, 0))
        results[h] = call(
            functools.partial(middle_kernel, GO[h], COME[h]), (4,),
            [near_spec] * 4 + [far_spec] * 3 + [rows_spec, w_spec],
            [far_spec] * 4 + [rows_spec, g_spec],
            [group] * 4 + [shape((8, 16, 4, 8, TT))] + [shape((4, 2, 16, 8, hidden), F32)],
            [pltpu.VMEM((128, hidden), F32)] * 2,
            12 * 4 * 128 * hidden * tok_dev // 2, 20 * 2**20,
        )(who, *arrived[h], back[h], w_far if h else w_own)
    returned = {h: two_stage(results[h][:4], COME[h]) for h in order}
    acts = {h: spread(results[h][4]) for h in order}

    near_spec = pl.BlockSpec((1, 4, PAIR, 8, TT), lambda e, t, w: (0, 0, t, 0, 0))
    far_spec = pl.BlockSpec((4, 4, PAIR, 8, TT), lambda e, t, w: (0, 0, t, 0, 0))
    tile_spec = pl.BlockSpec((512, PAIR * TT), lambda e, t, w: (0, (w[2] ^ e) * steps + t))
    whole_a = pl.BlockSpec((16, 32, width), lambda e, t, w: (0, 0, 0))
    input_grad, first = call(
        functools.partial(finish_kernel, COME), (2, steps),
        ([near_spec] * 4 + [far_spec] * 3) * 2 + [tile_spec, whole_a],
        [tile_spec, whole_a],
        [shape((512, tok_dev)), shape((16, 32, width), F32)],
        [pltpu.VMEM((512, 512), BF), pltpu.VMEM((512, 512), F32)],
        4 * 512 * 512 * tok_dev, 6 * 512 * tok_dev,
    )(who, *returned[0], *returned[1], inputs, a_one)

    layer_out, fourth = call(
        token_kernel, (16 // STEP,),
        [pl.BlockSpec((8, STEP, 4, 8, TT), lambda n, w: (0, (w[0] // STEP) ^ n, 0, 0, 0))] * 2 + [og_spec, a_spec],
        [og_spec, a_spec],
        [shape((8192, tok_part)), shape((2, 16, 8, 32, width), F32)], (),
        4 * 512 * 8192 * TT, 6 * 8192 * TT,
    )(who, acts[0], acts[1], output_grad, a_all)

    def both(mine):
        other = swap(mine)
        low, high = jnp.where(tok == 0, mine, other), jnp.where(tok == 0, other, mine)
        return jnp.concatenate([low, high], axis=0)

    kept = [results[h][5][:2] + swap(results[h][5][2:].astype(BF)).astype(F32) for h in (0, 1)]
    middle = both(kept[0] + flip(kept[1].astype(BF), 8).astype(F32)) * scale
    second = middle[:, 0].reshape(CB, 16, 2, CB, hidden).transpose(0, 2, 1, 3, 4).reshape(CB, width, hidden)
    third = middle[:, 1].reshape(CB, 16, 2, CB, hidden).transpose(0, 4, 2, 1, 3).reshape(CB, hidden, width)

    part = fourth[0] + swap(fourth[1].astype(BF)).astype(F32)
    part = part.reshape(4, 4, 8, 32, width)
    part = part[:, 0] + sum(flip(part[:, j].astype(BF), j).astype(F32) for j in (1, 2, 3))
    part = part[0] + sum(flip(part[j].astype(BF), 4 * j).astype(F32) for j in (1, 2, 3))
    fourth = both(part).reshape(16, CB, 2, CB, width) * scale
    fourth = fourth.transpose(3, 2, 0, 1, 4).reshape(CB, width, width)

    first = (first + swap(first)).reshape(16, CB, 2, CB, width) * scale
    first = first.transpose(3, 4, 2, 0, 1).reshape(CB, width, width)
    return (layer_out, input_grad, first, second, third, fourth)


def solution(mesh):
    placed = (
        P("feat", "tok"),
        P("feat", None, None),
        P("feat", None, None),
        P("feat", None, None),
        P("feat", None, None),
        P(None, ("tok", "feat")),
    )

    def local(inputs, first_weight, second_weight, third_weight, fourth_weight, output_grad):
        fits = (
            mesh.shape["feat"] == 16
            and mesh.shape["tok"] == 2
            and first_weight.shape == (CB, 128, 128)
            and output_grad.shape == (8192, TT)
            and inputs.shape[1] == 16 * TT
        )
        run = local_halves if fits else local_any
        return run(inputs, first_weight, second_weight, third_weight, fourth_weight, output_grad)

    return jax.shard_map(
        local,
        mesh=mesh,
        in_specs=placed,
        out_specs=(
            P(None, ("tok", "feat")),
            P("feat", "tok"),
            P("feat", None, None),
            P("feat", None, None),
            P("feat", None, None),
            P("feat", None, None),
        ),
        check_vma=False,
    )
```
